128 devices in a mesh: row: 8 (over x, core), col: 16 (over y, z).
Axes of the slice: x: 4, y: 4, z: 4, core: 2. Of those that a mesh axis runs over, the one named last changes fastest.
Arguments:
- child_update: bfloat16 [8, 8, 256, 2, 4096], P('row', None, None, None, 'col'), may hold values from -0.41992188 to 0.41992188
- front: float32 [12288, 12288], P('row', 'col')
- pivot_inverses: bfloat16 [8, 256, 256], replicated
- child_maps: int32 [2, 32], replicated, may hold values from 0 to 47, as said below
Outputs:
- front_out: float32 [12288, 12288], P('row', 'col')
- factor: bfloat16 [12288, 2048], P('row', 'col')
The draws below stay inside these ranges and needn't reach their ends.
Inputs may be any that keep to these rules, and one draw needn't show every extreme that they name: Each row of child_maps is strictly increasing, and holds every one of the 6 parent tiles g * 6 .. (g + 1) * 6 - 1 for some g.
All inputs are finite; a program needn't handle non-finite values.
Results may differ from the reference program's by a relative error of at most 0.033.
Values may be sent and summed in bfloat16 or wider, within the bound.
A program may use at most 192 MiB of HBM per device.

```python
import math
import jax
import jax.numpy as jnp

FR = 12288
TILE = 256
NPB = 8
PT = 48
CT = 32
RTILES = 8
CSPAN = 2
PT_ROW = 6
N_ROW = 8
N_COL = 16


def draw_child_maps(key, part):
    result = []
    for child_idx in range(2):
        child_key = jax.random.fold_in(key, 11 + child_idx)
        group_key, shuffle_key = jax.random.split(child_key)
        group_id = jax.random.randint(group_key, (), 0, PT // PT_ROW)
        shuffle = jax.random.permutation(shuffle_key, PT).astype(jnp.int32)
        tile_ids = jnp.arange(PT, dtype=jnp.int32)
        inside = tile_ids // PT_ROW == group_id
        scores = jnp.where(inside, shuffle - PT, shuffle)
        rank_of = jnp.argsort(jnp.argsort(scores))
        chosen_mask = rank_of < CT
        positions = jnp.nonzero(chosen_mask, size=CT)[0].astype(jnp.int32)
        result.append(positions)
    return jnp.stack(result, axis=0)


def draw_front(key, part):
    noise_key, diag_key = jax.random.split(jax.random.fold_in(key, 5))
    noise = 0.07 * jax.random.normal(noise_key, (FR, FR), jnp.float32)
    diagonal = 4.0 * jax.random.uniform(diag_key, (FR,), jnp.float32, 0.8, 1.25)
    row_ids = jnp.arange(FR)[:, None]
    col_ids = jnp.arange(FR)[None, :]
    return noise + jnp.where(row_ids == col_ids, diagonal[:, None], 0.0)


def draw_pivot_inverses(key, part):
    noise_key, diag_key = jax.random.split(jax.random.fold_in(key, 7))
    spread = 0.3 / math.sqrt(TILE)
    noise = spread * jax.random.normal(noise_key, (NPB, TILE, TILE), jnp.float32)
    diagonal = jax.random.uniform(diag_key, (NPB, TILE), jnp.float32, 0.8, 1.25)
    row_ids = jnp.arange(TILE)[:, None]
    col_ids = jnp.arange(TILE)[None, :]
    matrix = noise + jnp.where(row_ids == col_ids, diagonal[:, :, None], 0.0)
    return (0.25 * matrix).astype(jnp.bfloat16)


def shard_levels(own_key, extent, shards, least, top_value):
    loudness = 1.0
    for position, blocks in shards:
        draws = jax.random.uniform(jax.random.fold_in(jax.random.fold_in(own_key, 6), position), (blocks,), jnp.float32, least / len(shards), top_value / len(shards))
        loudness = loudness * jnp.repeat(jnp.exp(draws), extent[position] // blocks).reshape((-1,) + (1,) * (len(extent) - 1 - position))
    return loudness


def normal_values(own_key, dims, scale, limit, cuts=(), kind=jnp.bfloat16):
    values = scale * jax.random.normal(own_key, dims, jnp.float32)
    if cuts:
        values = values * shard_levels(own_key, dims, cuts, -0.22, 0.18)
    return jnp.clip(values, -limit, limit).astype(kind)


def setup_inputs(seed: int = 0) -> dict:
    streams_of = jax.random.split(jax.random.key(seed), 5)
    return {
        "child_update": normal_values(streams_of[0], (N_ROW, RTILES, TILE, CSPAN, N_COL * TILE), 0.07, 0.41992188, ((0, 8), (4, 16))),
        "front": draw_front(jax.random.fold_in(streams_of[4], 71), 0),
        "pivot_inverses": draw_pivot_inverses(jax.random.fold_in(streams_of[4], 71), 0),
        "child_maps": draw_child_maps(jax.random.fold_in(streams_of[4], 71), 0),
    }


def reference(child_update, front, pivot_inverses, child_maps):
    row_step = N_ROW // 2
    pieces = child_update.reshape(2, row_step, CT // row_step, TILE, CT // N_COL, N_COL, TILE)
    pieces = pieces.transpose(0, 2, 1, 4, 5, 3, 6).reshape(2, CT, CT, TILE, TILE)
    tiled_front = front.reshape(PT, TILE, PT, TILE).transpose(0, 2, 1, 3)
    for child_idx in range(2):
        mapping = child_maps[child_idx]
        tiled_front = tiled_front.at[mapping[:, None], mapping[None, :]].add(pieces[child_idx].astype(jnp.float32))
    current = tiled_front.transpose(0, 2, 1, 3).reshape(FR, FR)
    blocks = []
    for block_idx in range(NPB):
        start_col = block_idx * TILE
        column_panel = current[:, start_col:start_col + TILE].astype(jnp.bfloat16)
        row_panel = current[start_col:start_col + TILE, :].astype(jnp.bfloat16)
        factor_block = jnp.dot(column_panel, pivot_inverses[block_idx], preferred_element_type=jnp.float32).astype(jnp.bfloat16)
        current = current - jnp.dot(factor_block, row_panel, preferred_element_type=jnp.float32)
        blocks.append(factor_block)
    return current, jnp.concatenate(blocks, axis=1)
```

```python
import functools

import jax
import jax.numpy as jnp
from jax import lax
from jax.experimental import pallas as pl
from jax.experimental.pallas import tpu as pltpu
from jax.sharding import PartitionSpec as P

MESH = pl.DeviceIdType.MESH
BF = jnp.bfloat16
F32 = jnp.float32
HBM = pl.BlockSpec(memory_space=pl.ANY)
VM = pl.BlockSpec(memory_space=pltpu.VMEM)
SM = pl.BlockSpec(memory_space=pltpu.SMEM)
DMA = pltpu.SemaphoreType.DMA


def sds(shape, dtype):
    return jax.ShapeDtypeStruct(shape, dtype)


def pack_kernel(maps, strips, out):
    r = lax.axis_index("row")
    k, s = r // 4, r % 4
    for x in range(4):
        start = jnp.int32(0)
        for i in range(8):
            start += (maps[k, s + 4 * i] < 12 * x).astype(jnp.int32)
        for slot in range(3):
            idx = jnp.minimum(start + slot, 7)
            for core in range(2):
                out[x, core, :, slot] = strips[idx, :, core]


def pack(maps, strips):
    return pl.pallas_call(
        pack_kernel,
        out_shape=sds((4, 2, 16, 3, 8, 512), BF),
        in_specs=[SM, VM],
        out_specs=VM,
        compiler_params=pltpu.CompilerParams(vmem_limit_bytes=24 << 20),
    )(maps, strips)


def front_kernel(fb, fl, lsem, ssem, rsem):
    r, c = lax.axis_index("row"), lax.axis_index("col")
    x, core = r // 2, r % 2
    me = c * 2 + core
    bar = pltpu.get_barrier_semaphore()

    def greet(i, n):
        d = lax.rem(me + i, 32)
        pl.semaphore_signal(
            bar, inc=1, device_id=(2 * x + lax.rem(d, 2), d // 2), device_id_type=MESH
        )
        return n

    lax.fori_loop(1, 32, greet, 0)
    pl.semaphore_wait(bar, 31)

    @pl.when(c < 3)
    def _():
        loc = pltpu.make_async_copy(
            fb.at[:, me], fl.at[jnp.minimum(c, 2), pl.ds(6 * core, 6)], lsem
        )
        loc.start()

        def send(i, n):
            d = lax.rem(me + i, 32)
            pltpu.make_async_remote_copy(
                fb.at[:, d],
                fl.at[jnp.minimum(c, 2), pl.ds(6 * core, 6)],
                ssem,
                rsem,
                device_id=(2 * x + lax.rem(d, 2), d // 2),
                device_id_type=MESH,
            ).start()
            return n

        lax.fori_loop(1, 32, send, 0)
        loc.wait()

        done = fb.at[:, pl.ds(0, 31)]
        pltpu.make_async_remote_copy(
            done, done, ssem, rsem, device_id=(r, c), device_id_type=MESH
        ).wait_send()
        part = fl.at[:, pl.ds(0, 10)]
        pltpu.make_async_remote_copy(
            part, part, ssem, rsem, device_id=(r, c), device_id_type=MESH
        ).wait_recv()

    @pl.when(c >= 3)
    def _():
        pltpu.make_async_remote_copy(
            fl, fl, ssem, rsem, device_id=(r, c), device_id_type=MESH
        ).wait_recv()


def front_scatter(fb):
    return pl.pallas_call(
        front_kernel,
        out_shape=sds((3, 12, 8, 768), BF),
        in_specs=[HBM],
        out_specs=HBM,
        scratch_shapes=[DMA, DMA, DMA],
        compiler_params=pltpu.CompilerParams(collective_id=1, has_side_effects=True),
    )(fb)


def sum_kernel(maps, recv, fl, cs, al, inv, rowt, cnt):
    x = lax.axis_index("row") // 2
    for k in range(2):

        def clear(t, n):
            inv[k, t] = -1
            return n

        lax.fori_loop(0, 48, clear, 0)

        def fill(a, n):
            inv[k, maps[k, a]] = a
            return n

        lax.fori_loop(0, 32, fill, 0)
        for s in range(4):
            start = jnp.int32(0)
            for i in range(8):
                start += (maps[k, s + 4 * i] < 12 * x).astype(jnp.int32)
            cnt[s] = start
        for pr in range(12):
            a = inv[k, 12 * x + pr]
            held = jnp.maximum(a, 0)
            s = held % 4
            rowt[k, pr] = jnp.where(a >= 0, (k * 4 + s) * 48 + held // 4 - cnt[s], -1)

    def column(pc, n):
        col = pl.ds(pl.multiple_of(pc * 256, 256), 256)
        b = [inv[k, pc] for k in range(2)]
        held = [jnp.maximum(v, 0) for v in b]
        for pr in range(12):
            total = None
            for k in range(2):
                row = rowt[k, pr]
                ok = (row >= 0) & (b[k] >= 0)
                idx = jnp.maximum(row, 0) + (held[k] % 16) * 3
                half = pl.multiple_of((held[k] // 16) * 256, 256)
                v = recv[idx, :, pl.ds(half, 256)].astype(F32)
                v = v * jnp.where(ok, 1.0, 0.0)
                total = v if total is None else total + v
            cs[pr, :, col] = total.astype(BF)
        return n

    lax.fori_loop(0, 48, column, 0)
    for c0 in range(3):
        w = min(768, 2048 - 768 * c0)
        for pr in range(12):
            part = cs[pr, :, 768 * c0 : 768 * c0 + w].astype(F32)
            al[pr, :, 768 * c0 : 768 * c0 + w] = (part + fl[c0, pr, :, :w].astype(F32)).astype(BF)


def child_sums(maps, recv, fl):
    return pl.pallas_call(
        sum_kernel,
        out_shape=(sds((12, 8, 12288), BF), sds((12, 8, 2048), BF)),
        in_specs=[SM, VM, VM],
        out_specs=(VM, VM),
        scratch_shapes=[
            pltpu.SMEM((2, 48), jnp.int32),
            pltpu.SMEM((2, 12), jnp.int32),
            pltpu.SMEM((4,), jnp.int32),
        ],
        compiler_params=pltpu.CompilerParams(vmem_limit_bytes=40 << 20),
    )(maps, recv, fl)


def exchange_kernel(cs, al, recv, blk, lsem, psem, prem, lsend, lrecv, csend, crecv):
    r, c = lax.axis_index("row"), lax.axis_index("col")
    x, core = r // 2, r % 2
    me = c * 2 + core
    bar = pltpu.get_barrier_semaphore()

    def greet(i, n):
        d = lax.rem(me + i, 32)
        pl.semaphore_signal(
            bar, inc=1, device_id=(2 * x + lax.rem(d, 2), d // 2), device_id_type=MESH
        )
        return n

    lax.fori_loop(1, 32, greet, 0)
    for dx in range(1, 4):
        for rho in range(2):
            pl.semaphore_signal(
                bar, inc=1, device_id=(2 * lax.rem(x + dx, 4) + rho, c), device_id_type=MESH
            )
    pl.semaphore_wait(bar, 31 + 6)

    def corner(rho, h, dev, to):
        return pltpu.make_async_remote_copy(
            al.at[pl.ds(4 * rho + 2 * h, 2)],
            blk.at[h, pl.ds(3, 2), pl.ds(pl.multiple_of(8 * core, 8), 8)],
            csend.at[to, h],
            crecv.at[core, h],
            device_id=dev,
            device_id_type=MESH,
        )

    def corner_from(frm, h):
        return pltpu.make_async_remote_copy(
            al.at[pl.ds(0, 2)],
            blk.at[h, pl.ds(3, 2), pl.ds(8 * frm, 8)],
            csend.at[0, h],
            crecv.at[frm, h],
            device_id=(r, c),
            device_id_type=MESH,
        )

    @pl.when(x == 0)
    def _():
        for dx in range(1, 4):
            for rho in range(2):
                for h in range(2):
                    corner(rho, h, (2 * dx + rho, c), 2 * dx + rho).start()
        for h in range(2):
            corner(1 - core, h, (1 - core, c), 0).start()
            pltpu.make_async_copy(
                al.at[pl.ds(4 * core + 2 * h, 2)],
                blk.at[h, pl.ds(3, 2), pl.ds(pl.multiple_of(8 * core, 8), 8)],
                lsem.at[2 + h],
            ).start()

    rows = pl.ds(pl.multiple_of(8 * core, 8), 8)
    swaps, keeps = [], []
    for h in range(2):
        cp = pltpu.make_async_remote_copy(
            al.at[pl.ds(6 * (1 - core) + 3 * h, 3)],
            blk.at[h, pl.ds(0, 3), rows],
            lsend.at[h],
            lrecv.at[h],
            device_id=(2 * x + 1 - core, c),
            device_id_type=MESH,
        )
        cp.start()
        swaps.append(cp)
        cp = pltpu.make_async_copy(
            al.at[pl.ds(6 * core + 3 * h, 3)], blk.at[h, pl.ds(0, 3), rows], lsem.at[h]
        )
        cp.start()
        keeps.append(cp)

    def mine(rho, d):
        return cs.at[pl.ds(6 * rho, 6), :, pl.ds(pl.multiple_of((d // 2) * 768, 768), 768)]

    own = pltpu.make_async_copy(mine(core, me), recv.at[:, me], lsem.at[4])
    own.start()

    def send(i, n):
        d = lax.rem(me + i, 32)
        rho = lax.rem(d, 2)
        pltpu.make_async_remote_copy(
            mine(rho, d),
            recv.at[:, me],
            psem,
            prem,
            device_id=(2 * x + rho, d // 2),
            device_id_type=MESH,
        ).start()
        return n

    lax.fori_loop(1, 32, send, 0)

    for cp in keeps:
        cp.wait()
    for cp in swaps:
        cp.wait()
    own.wait()

    @pl.when(x == 0)
    def _():
        for dx in range(1, 4):
            for rho in range(2):
                for h in range(2):
                    corner(rho, h, (2 * dx + rho, c), 2 * dx + rho).wait_send()
        for h in range(2):
            corner(1 - core, h, (1 - core, c), 0).wait_send()
            pltpu.make_async_copy(
                al.at[pl.ds(4 * core + 2 * h, 2)],
                blk.at[h, pl.ds(3, 2), pl.ds(pl.multiple_of(8 * core, 8), 8)],
                lsem.at[2 + h],
            ).wait()

    for frm in range(2):

        @pl.when((x > 0) | (core != frm))
        def _():
            for h in range(2):
                corner_from(frm, h).wait_recv()

    done = recv.at[:, pl.ds(0, 31)]
    pltpu.make_async_remote_copy(
        done, done, psem, prem, device_id=(r, c), device_id_type=MESH
    ).wait()


def exchange(cs, al):
    return pl.pallas_call(
        exchange_kernel,
        out_shape=(sds((6, 32, 8, 768), BF), sds((2, 5, 16, 2048), BF)),
        in_specs=[HBM, HBM],
        out_specs=(HBM, HBM),
        scratch_shapes=[
            DMA((5,)), DMA, DMA, DMA((2,)), DMA((2,)), DMA((8, 2)), DMA((2, 2)),
        ],
        compiler_params=pltpu.CompilerParams(collective_id=2, has_side_effects=True),
    )(cs, al)


def gather_kernel(blk, ar, g, gs, rg, lsem, s1, r1, s2, r2, ssib, rsib, sx, rx, sxs, rxs):
    r, c = lax.axis_index("row"), lax.axis_index("col")
    x, core = r // 2, r % 2
    y, z = c // 4, c % 4
    bar = pltpu.get_barrier_semaphore()
    sib = (2 * x + 1 - core, c)

    def cid(h, df, ds):
        dy, dz = (ds, df) if h == 0 else (df, ds)
        return lax.rem(y + dy + 4, 4) * 4 + lax.rem(z + dz + 4, 4)

    def xdev(dx):
        return (2 * lax.rem(x + dx + 4, 4) + core, c)

    partners = [sib, xdev(1), xdev(-1)]
    for d in (1, -1):
        partners += [(r, cid(0, d, 0)), (r, cid(0, 0, d))]
    for dev in partners:
        pl.semaphore_signal(bar, inc=1, device_id=dev, device_id_type=MESH)
    pl.semaphore_wait(bar, len(partners))

    sent = []

    def push(src, dst, ss, rs, dev):
        cp = pltpu.make_async_remote_copy(
            src, dst, ss, rs, device_id=dev, device_id_type=MESH
        )
        cp.start()
        sent.append(cp)

    def landed(dst, ss, rs):
        pltpu.make_async_remote_copy(
            dst, dst, ss, rs, device_id=sib, device_id_type=MESH
        ).wait_recv()

    locs = []
    for h in range(2):
        cp = pltpu.make_async_copy(blk.at[h], g.at[c, h], lsem.at[h])
        cp.start()
        locs.append(cp)

    cols = [pl.ds(0, 1024), pl.ds(1024, 1024)]
    order = (0, -1, 1, 2)

    def first(h):
        for n, d in enumerate((1, -1)):
            push(blk.at[h], g.at[c, h], s1.at[h, n], r1.at[h, n], (r, cid(h, d, 0)))

    def second(h, f):
        df = order[f]
        ident = cid(h, df, 0)
        src = blk.at[h] if df == 0 else g.at[ident, h]
        for n, d in enumerate((1, -1)):
            push(src, g.at[ident, h], s2.at[h, f, n], r2.at[h, f, n], (r, cid(h, 0, d)))

    def sibling(h, df, ds, n, own=False):
        ident = cid(h, df, ds)
        src = blk.at[h, pl.ds(3, 2)] if own else g.at[ident, h, pl.ds(3, 2)]
        push(src, gs.at[ident, h], ssib.at[h, n], rsib.at[h, n], sib)

    def relay_first(h, n):
        ident = cid(h, -1 if n == 0 else 1, 0)
        landed(g.at[ident, h], s1.at[h, n], r1.at[h, n])
        part = g.at[ident, h, :, :, cols[n]]
        push(part, part, s1.at[h, 2 + n], r1.at[h, 2 + n], (r, cid(h, 1 if n == 0 else -1, 0)))
        second(h, 1 + n)
        sibling(h, -1 if n == 0 else 1, 0, 1 + n)

    def finish_first(h):
        ident = cid(h, 2, 0)
        for n in range(2):
            landed(g.at[ident, h, :, :, cols[n]], s1.at[h, 2 + n], r1.at[h, 2 + n])
        second(h, 3)
        sibling(h, 2, 0, 3)

    def relay_second(h, f, n):
        ds = -1 if n == 0 else 1
        ident = cid(h, order[f], ds)
        landed(g.at[ident, h], s2.at[h, f, n], r2.at[h, f, n])
        part = g.at[ident, h, :, :, cols[n]]
        push(
            part, part, s2.at[h, f, 2 + n], r2.at[h, f, 2 + n],
            (r, cid(h, 0, 1 if n == 0 else -1)),
        )
        sibling(h, order[f], ds, 4 + 3 * f + n)

    def finish_second(h, f):
        ident = cid(h, order[f], 2)
        for n in range(2):
            landed(g.at[ident, h, :, :, cols[n]], s2.at[h, f, 2 + n], r2.at[h, f, 2 + n])
        sibling(h, order[f], 2, 4 + 3 * f + 2)

    for h in range(2):
        first(h)
    for h in range(2):
        second(h, 0)
        sibling(h, 0, 0, 0, own=True)

    def chunk(q):
        return rg.at[pl.ds(pl.multiple_of(512 * q, 512), 512)]

    def xcopy(src, dst, ss, rs, dev):
        return pltpu.make_async_remote_copy(
            src, dst, ss, rs, device_id=dev, device_id_type=MESH
        )

    def arow(q):
        return ar.at[pl.ds(512 * q, 512)]

    def zero_core0():
        out = [xcopy(arow(2), chunk(2), sxs.at[2], rxs.at[2], sib)]
        for u in range(2):
            for n, d in enumerate((1, -1)):
                out.append(xcopy(arow(u), chunk(u), sx.at[n, u], rx.at[u], xdev(d)))
            out.append(xcopy(arow(u), chunk(u), sxs.at[u], rxs.at[u], sib))
        return out

    def zero_core1():
        out = [
            xcopy(arow(0), chunk(3), sx.at[n, 1], rx.at[1], xdev(d))
            for n, d in enumerate((1, -1))
        ]
        out.append(xcopy(arow(0), chunk(3), sxs.at[1], rxs.at[1], sib))
        return out

    def zero_core1_late():
        return [
            xcopy(chunk(2), chunk(2), sx.at[n, 0], rx.at[0], xdev(d))
            for n, d in enumerate((1, -1))
        ]

    @pl.when((x == 0) & (core == 0))
    def _():
        pltpu.make_async_copy(ar, rg.at[pl.ds(0, 1536)], lsem.at[2]).start()
        for cp in zero_core0():
            cp.start()

    @pl.when((x == 0) & (core == 1))
    def _():
        pltpu.make_async_copy(arow(0), chunk(3), lsem.at[2]).start()
        for cp in zero_core1():
            cp.start()

    for n in range(2):
        for h in range(2):
            relay_first(h, n)

    @pl.when((x == 0) & (core == 1))
    def _():
        landed(chunk(2), sxs.at[2], rxs.at[2])
        for cp in zero_core1_late():
            cp.start()

    for n in range(2):
        for h in range(2):
            relay_second(h, 0, n)
    for h in range(2):
        finish_first(h)

    mine = 2 * core

    def onward(u):
        return xcopy(
            chunk(mine + u), chunk(mine + u), sx.at[0, u], rx.at[u], xdev(1 if u == 0 else -1)
        )

    def across(u):
        return xcopy(chunk(mine + u), chunk(mine + u), sxs.at[u], rxs.at[u], sib)

    for u, via in ((1, 3), (0, 1)):

        @pl.when((x == 1) | (x == 3))
        def _():
            landed(chunk(mine + u), sx.at[0, u], rx.at[u])
            across(u).start()

        @pl.when(x == via)
        def _():
            onward(u).start()

    for f in (1, 2):
        for n in range(2):
            for h in range(2):
                relay_second(h, f, n)
    for h in range(2):
        finish_second(h, 0)
    for n in range(2):
        for h in range(2):
            relay_second(h, 3, n)
    for f in (1, 2, 3):
        for h in range(2):
            finish_second(h, f)

    @pl.when(x == 2)
    def _():
        for u in range(2):
            landed(chunk(mine + u), sx.at[0, u], rx.at[u])
            across(u).start()

    @pl.when(x > 0)
    def _():
        for u in range(2):
            across(u).wait_send()
            landed(chunk(2 - mine + u), sxs.at[u], rxs.at[u])

    for u, via in ((0, 1), (1, 3)):

        @pl.when(x == via)
        def _():
            onward(u).wait_send()

    @pl.when((x == 0) & (core == 0))
    def _():
        pltpu.make_async_copy(ar, rg.at[pl.ds(0, 1536)], lsem.at[2]).wait()
        for cp in zero_core0():
            cp.wait_send()
        landed(chunk(3), sxs.at[1], rxs.at[1])

    @pl.when((x == 0) & (core == 1))
    def _():
        pltpu.make_async_copy(arow(0), chunk(3), lsem.at[2]).wait()
        for cp in zero_core1() + zero_core1_late():
            cp.wait_send()
        for u in range(2):
            landed(chunk(u), sxs.at[u], rxs.at[u])

    for cp in locs:
        cp.wait()
    for cp in sent:
        cp.wait_send()
    for h in range(2):
        for n, (df, ds) in enumerate(
            [(0, 0), (-1, 0), (1, 0), (2, 0)]
            + [(df, ds) for df in order for ds in (-1, 1, 2)]
        ):
            landed(gs.at[cid(h, df, ds), h], ssib.at[h, n], rsib.at[h, n])


def gather(blk, ar):
    return pl.pallas_call(
        gather_kernel,
        out_shape=(
            sds((16, 2, 5, 16, 2048), BF),
            sds((16, 2, 2, 16, 2048), BF),
            sds((2048, 768), BF),
        ),
        in_specs=[HBM, HBM],
        out_specs=(HBM, HBM, HBM),
        scratch_shapes=[
            DMA((3,)),
            DMA((2, 4)), DMA((2, 4)),
            DMA((2, 4, 4)), DMA((2, 4, 4)),
            DMA((2, 16)), DMA((2, 16)),
            DMA((2, 2)), DMA((2,)),
            DMA((3,)), DMA((3,)),
        ],
        compiler_params=pltpu.CompilerParams(collective_id=3, has_side_effects=True),
    )(blk, ar)


def eliminate_kernel(g, gs, rg, cs, front, pinv, out, factor, xs, rr, sem):
    r, c = lax.axis_index("row"), lax.axis_index("col")
    core = r % 2
    loads = []
    for pr in range(8):
        h, u = (pr % 4) // 2, pr % 2
        for src, side in ((g, pr // 4), (gs, 1 - pr // 4)):
            unit = 3 + u if src is g else u

            @pl.when(core == side)
            def _():
                pltpu.make_async_copy(src.at[:, h, unit], xs.at[pr], sem.at[pr]).start()

    for t in range(6):
        pltpu.make_async_copy(g.at[:, t // 3, t % 3], xs.at[8 + t], sem.at[8 + t]).start()
    pltpu.make_async_copy(rg, rr, sem.at[14]).start()
    for t in range(14):
        pltpu.make_async_copy(g.at[:, 0, 0], xs.at[t], sem.at[t]).wait()
    pltpu.make_async_copy(rg, rr, sem.at[14]).wait()

    def rows(t, lo, hi):
        return xs[t, :, :, lo:hi].reshape(256, hi - lo)

    for j in range(8):
        lo, hi = 256 * j, 256 * (j + 1)

        def panel(t, n):
            acc = rows(t, lo, hi).astype(F32)
            if j:
                upper = xs[0:j, :, :, lo:hi].reshape(lo, 256)
                acc = acc - jnp.dot(rows(t, 0, lo), upper, preferred_element_type=F32)
            block = jnp.dot(acc.astype(BF), pinv[j], preferred_element_type=F32)
            xs[t, :, :, lo:hi] = block.astype(BF).reshape(16, 16, 256)
            return n

        lax.fori_loop(j + 1, 14, panel, 0)
        if j:
            left = rows(j, 0, lo)
            for m in range(j + 1, 8):
                cols = slice(256 * m, 256 * (m + 1))
                acc = rows(j, 256 * m, 256 * (m + 1)).astype(F32)
                upper = xs[0:j, :, :, cols].reshape(lo, 256)
                acc = acc - jnp.dot(left, upper, preferred_element_type=F32)
                xs[j, :, :, cols] = acc.astype(BF).reshape(16, 16, 256)
            acc = rr[lo:hi].astype(F32) - jnp.dot(left, rr[0:lo], preferred_element_type=F32)
            rr[lo:hi] = acc.astype(BF)

    mycols = pl.ds(pl.multiple_of(c * 128, 128), 128)

    def update(t, n):
        at = pl.ds(pl.multiple_of(t * 256, 256), 256)
        prod = jnp.dot(rows(8 + t, 0, 2048), rr[...], preferred_element_type=F32)
        out[at, :] = front[at, :] + cs[at, :].astype(F32) - prod
        factor[at, :] = xs[8 + t, :, :, mycols].reshape(256, 128)
        return n

    lax.fori_loop(0, 6, update, 0)


def eliminate(g, gs, rg, cs, front, pinv):
    return pl.pallas_call(
        eliminate_kernel,
        out_shape=(sds((1536, 768), F32), sds((1536, 128), BF)),
        in_specs=[HBM, HBM, HBM, VM, VM, VM],
        out_specs=(VM, VM),
        scratch_shapes=[
            pltpu.VMEM((14, 16, 16, 2048), BF),
            pltpu.VMEM((2048, 768), BF),
            DMA((15,)),
        ],
        compiler_params=pltpu.CompilerParams(vmem_limit_bytes=60 << 20),
    )(g, gs, rg, cs, front, pinv)


def per_device(child_update, front, pivot_inverses, child_maps):
    strips = child_update[0].reshape(8, 16, 2, 8, 512)
    send = pack(child_maps, strips)
    fb = front.astype(BF).reshape(6, 32, 8, 768)
    recv = lax.all_to_all(
        send.reshape(128, 3, 8, 512), ("row", "col"), split_axis=0, concat_axis=0, tiled=True
    )
    fl = front_scatter(fb)
    cs, al = child_sums(child_maps, recv.reshape(384, 8, 512), fl)
    own, blk = exchange(cs, al)
    own = own.reshape(1536, 768)
    ar = (front + own.astype(F32)).astype(BF)
    g, gs, rg = gather(blk, ar)
    return eliminate(g, gs, rg, own, front, pivot_inverses)


def solution(mesh):
    placed = (P("row", None, None, None, "col"), P("row", "col"), P(), P())
    return jax.shard_map(
        per_device,
        mesh=mesh,
        in_specs=placed,
        out_specs=(P("row", "col"), P("row", "col")),
        check_vma=False,
    )
```
